32 devices in a mesh: ctx: 8 (over z, x), head: 4 (over y, core).
Axes of the slice: x: 2, y: 2, z: 4, core: 2. Of those that a mesh axis runs over, the one named last changes fastest.
Arguments:
- queries: bfloat16 [4096, 4096], P('ctx', 'head'), may hold values from -5 to 5
- keys: bfloat16 [4096, 512], P('ctx', 'head'), may hold values from -5 to 5
- values: bfloat16 [4096, 512], P('ctx', 'head'), may hold values from -8 to 8
- feature_map: bfloat16 [4, 128, 16], P('head'), may hold values from -0.5 to 0.5
- out_proj: bfloat16 [4096, 8192], P('ctx', 'head'), may hold values from -0.09375 to 0.09375
- teacher: bfloat16 [4096, 8192], P('ctx', 'head'), may hold values from -16 to 16
Outputs:
- student_out: bfloat16 [4096, 8192], P('ctx', 'head')
- loss: float32 [], replicated
- feature_grad: float32 [4, 128, 16], P('head')
The draws below stay inside these ranges and needn't reach their ends.
All inputs are finite; a program needn't handle non-finite values.
Results may differ from the reference program's by a relative error of at most 0.006.
Values may be sent and summed in bfloat16 or wider, within the bound.
A program may use at most 128 MiB of HBM per device.

```python
import math
import jax
import jax.numpy as jnp
from jax import lax

D = 8192
HEAD_DIM = 128
GROUP = 8
KV_HEADS = 4
Q_HEADS = 32
COL_DEV = 2048
FEAT = 16
WIN = 64
TOK_DEV = 512
LENGTH = 4096


def draw_queries(key, part):
    drawn = jax.random.normal(jax.random.fold_in(key, 11), (LENGTH, KV_HEADS, GROUP, HEAD_DIM), jnp.float32)
    return jnp.clip(drawn, -5.0, 5.0).reshape(LENGTH, Q_HEADS * HEAD_DIM).astype(jnp.bfloat16)


def draw_keys(key, part):
    drawn = jax.random.normal(jax.random.fold_in(key, 21), (LENGTH, KV_HEADS, HEAD_DIM), jnp.float32)
    return jnp.clip(drawn, -5.0, 5.0).reshape(LENGTH, KV_HEADS * HEAD_DIM).astype(jnp.bfloat16)


def draw_values(key, part):
    region = max(TOK_DEV // 2, 1)
    region_count = LENGTH // region
    offsets = jax.random.normal(jax.random.fold_in(key, 41), (region_count, 1, KV_HEADS * HEAD_DIM), jnp.float32) * 1.5
    jitter = jax.random.normal(jax.random.fold_in(key, 42), (region_count, region, KV_HEADS * HEAD_DIM), jnp.float32)
    return jnp.clip(offsets + jitter, -8.0, 8.0).reshape(LENGTH, KV_HEADS * HEAD_DIM).astype(jnp.bfloat16)


def draw_teacher(key, part):
    position = jnp.arange(LENGTH, dtype=jnp.float32)
    rising = 1.0 + 2.0 * position / LENGTH
    drawn = jnp.clip(jax.random.normal(jax.random.fold_in(key, 51), (LENGTH, D), jnp.float32), -4.0, 4.0)
    return jnp.clip(drawn * rising[:, None], -16.0, 16.0).astype(jnp.bfloat16)


def steps_of(rng, dims, split, smallest, top_value):
    gain = 1.0
    for axis_at, parts in split:
        heights = jax.random.uniform(jax.random.fold_in(jax.random.fold_in(rng, 6), axis_at), (parts,), jnp.float32, smallest / len(split), top_value / len(split))
        gain = gain * jnp.repeat(jnp.exp(heights), dims[axis_at] // parts).reshape((-1,) + (1,) * (len(dims) - 1 - axis_at))
    return gain


def normal_values(rng, shape, scale, reach, split=(), kind=jnp.bfloat16):
    values = scale * jax.random.normal(rng, shape, jnp.float32)
    if split:
        values = values * steps_of(rng, shape, split, -0.22, 0.18)
    return jnp.clip(values, -reach, reach).astype(kind)


def setup_inputs(seed: int = 0) -> dict:
    splits = jax.random.split(jax.random.key(seed), 7)
    return {
        "queries": draw_queries(jax.random.fold_in(splits[6], 71), 0),
        "keys": draw_keys(jax.random.fold_in(splits[6], 71), 0),
        "values": draw_values(jax.random.fold_in(splits[6], 71), 0),
        "feature_map": normal_values(splits[3], (KV_HEADS, HEAD_DIM, FEAT), HEAD_DIM ** -0.5, 0.5, ((0, 4),)),
        "out_proj": normal_values(splits[4], (Q_HEADS * HEAD_DIM, D), (Q_HEADS * HEAD_DIM) ** -0.5, 0.09375, ((0, 8), (1, 4))),
        "teacher": draw_teacher(jax.random.fold_in(splits[6], 71), 0),
    }


exact_mode = lax.Precision.HIGHEST

def taylor_square(features):
    feature_count = features.shape[-1]
    outer = features[..., :, None] * features[..., None, :]
    return outer.reshape(features.shape[:-1] + (feature_count * feature_count,))

def taylor_linear(query_float, key_float, value_float, feature_weights):
    query_features = jnp.einsum('lgqe,gef->lgqf', query_float, feature_weights, precision=exact_mode)
    key_features = jnp.einsum('lge,gef->lgf', key_float, feature_weights, precision=exact_mode)
    blocks = LENGTH // TOK_DEV
    query_blocks = query_features.reshape(blocks, TOK_DEV, KV_HEADS, GROUP, FEAT)
    key_blocks = key_features.reshape(blocks, TOK_DEV, KV_HEADS, FEAT)
    value_blocks = value_float.reshape(blocks, TOK_DEV, KV_HEADS, HEAD_DIM)
    causal = lax.broadcasted_iota(jnp.int32, (TOK_DEV, TOK_DEV), 0) >= lax.broadcasted_iota(jnp.int32, (TOK_DEV, TOK_DEV), 1)
    initial = (jnp.zeros((KV_HEADS, FEAT * FEAT, HEAD_DIM), jnp.float32), jnp.zeros((KV_HEADS, FEAT, HEAD_DIM), jnp.float32), jnp.zeros((KV_HEADS, HEAD_DIM), jnp.float32), jnp.zeros((KV_HEADS, FEAT * FEAT), jnp.float32), jnp.zeros((KV_HEADS, FEAT), jnp.float32), jnp.zeros((KV_HEADS,), jnp.float32))

    def one_step(carried, block):
        past_square_v, past_linear_v, past_values, past_square_k, past_linear_k, past_count = carried
        query_block, key_block, value_block = block
        qk_inner = jnp.einsum('tgqf,sgf->gqts', query_block, key_block, precision=exact_mode) / 4.0
        kernel = jnp.where(causal, 1.0 + qk_inner + 0.5 * qk_inner * qk_inner, 0.0)
        numerator = jnp.einsum('gqts,sge->tgqe', kernel, value_block, precision=exact_mode)
        denominator = jnp.transpose(lax.optimization_barrier(jnp.sum(kernel, axis=-1)), (2, 0, 1))
        query_square = taylor_square(query_block)
        numerator = numerator + jnp.einsum('tgqk,gke->tgqe', query_square, past_square_v, precision=exact_mode) / 32.0 + jnp.einsum('tgqf,gfe->tgqe', query_block, past_linear_v, precision=exact_mode) / 4.0 + past_values[None, :, None, :]
        denominator = denominator + jnp.einsum('tgqk,gk->tgq', query_square, past_square_k, precision=exact_mode) / 32.0 + jnp.einsum('tgqf,gf->tgq', query_block, past_linear_k, precision=exact_mode) / 4.0 + past_count[None, :, None]
        key_square = taylor_square(key_block)
        updated = (past_square_v + jnp.einsum('sgk,sge->gke', key_square, value_block, precision=exact_mode), past_linear_v + jnp.einsum('sgf,sge->gfe', key_block, value_block, precision=exact_mode), past_values + lax.optimization_barrier(jnp.sum(value_block, axis=0)), past_square_k + lax.optimization_barrier(jnp.sum(key_square, axis=0)), past_linear_k + lax.optimization_barrier(jnp.sum(key_block, axis=0)), past_count + float(TOK_DEV))
        return (updated, numerator / denominator[..., None])
    finals, outputs = lax.scan(jax.checkpoint(one_step), initial, (query_blocks, key_blocks, value_blocks))
    return outputs.reshape(LENGTH, KV_HEADS, GROUP, HEAD_DIM)

def window_attention(query_heads, key_heads, value_heads):
    blocks = LENGTH // TOK_DEV
    pad_rows = jnp.zeros((WIN, KV_HEADS, HEAD_DIM), jnp.bfloat16)
    key_padded = jnp.concatenate([pad_rows, key_heads], 0)
    value_padded = jnp.concatenate([pad_rows, value_heads], 0)
    query_pos = lax.broadcasted_iota(jnp.int32, (TOK_DEV, TOK_DEV + WIN), 0)
    key_pos = lax.broadcasted_iota(jnp.int32, (TOK_DEV, TOK_DEV + WIN), 1)
    distance = query_pos + WIN - key_pos

    def one_block(block_id):
        first_row = (block_id * TOK_DEV).astype(jnp.int32)
        query_block = lax.dynamic_slice_in_dim(query_heads, first_row, TOK_DEV, 0)
        key_block = lax.dynamic_slice_in_dim(key_padded, first_row, TOK_DEV + WIN, 0)
        value_block = lax.dynamic_slice_in_dim(value_padded, first_row, TOK_DEV + WIN, 0)
        scores = jnp.einsum('tgqe,sge->gqts', query_block.astype(jnp.float32), key_block.astype(jnp.float32), precision=exact_mode) / math.sqrt(HEAD_DIM)
        allowed = (distance >= 0) & (distance < WIN) & (first_row + key_pos - WIN >= 0)
        scores = jnp.where(allowed, scores, -jnp.inf)
        row_max = lax.optimization_barrier(jnp.max(scores, axis=-1, keepdims=True))
        weights = jnp.where(allowed, jnp.exp(scores - row_max), 0.0)
        attn_weights = (weights / lax.optimization_barrier(jnp.sum(weights, axis=-1, keepdims=True))).astype(jnp.bfloat16)
        return jnp.einsum('gqts,sge->tgqe', attn_weights.astype(jnp.float32), value_block.astype(jnp.float32), precision=exact_mode)
    outputs = lax.map(one_block, jnp.arange(blocks, dtype=jnp.int32))
    return outputs.reshape(LENGTH, KV_HEADS, GROUP, HEAD_DIM)

def head_gradient(d_student, out_proj):
    column_blocks = D // COL_DEV

    def add_block(block_id, running):
        first_col = (block_id * COL_DEV).astype(jnp.int32)
        grad_cols = lax.dynamic_slice_in_dim(d_student, first_col, COL_DEV, 1)
        weight_cols = lax.dynamic_slice_in_dim(out_proj, first_col, COL_DEV, 1)
        partial_sum = lax.dot_general(grad_cols, weight_cols, (((1,), (1,)), ((), ())), preferred_element_type=jnp.float32)
        rounded = lax.optimization_barrier(partial_sum.astype(jnp.bfloat16))
        return running + rounded.astype(jnp.float32)
    start = jnp.zeros((LENGTH, Q_HEADS * HEAD_DIM), jnp.float32)
    return lax.fori_loop(jnp.int32(0), jnp.int32(column_blocks), add_block, start)

def reference(queries, keys, values, feature_map, out_proj, teacher):
    query_heads = queries.reshape(LENGTH, KV_HEADS, GROUP, HEAD_DIM)
    key_heads = keys.reshape(LENGTH, KV_HEADS, HEAD_DIM)
    value_heads = values.reshape(LENGTH, KV_HEADS, HEAD_DIM)
    window_out = window_attention(query_heads, key_heads, value_heads)
    query_float = query_heads.astype(jnp.float32)
    key_float = key_heads.astype(jnp.float32)
    value_float = value_heads.astype(jnp.float32)

    def linear_part(feature_weights):
        return taylor_linear(query_float, key_float, value_float, feature_weights)
    linear_out, pullback = jax.vjp(linear_part, feature_map.astype(jnp.float32))
    head_out = (linear_out + window_out).astype(jnp.bfloat16).reshape(LENGTH, Q_HEADS * HEAD_DIM)
    student_out = jnp.dot(head_out, out_proj, preferred_element_type=jnp.float32).astype(jnp.bfloat16)
    residual = student_out.astype(jnp.float32) - teacher.astype(jnp.float32)
    loss = jnp.sum(residual * residual) / (LENGTH * D)
    d_student = (2.0 * residual / LENGTH).astype(jnp.bfloat16)
    d_head = head_gradient(d_student, out_proj)
    grads = pullback(d_head.reshape(LENGTH, KV_HEADS, GROUP, HEAD_DIM))
    return (student_out, loss, grads[0])
```

```python
import functools
import math

import jax
import jax.numpy as jnp
from jax import lax
from jax.experimental import pallas as pl
from jax.experimental.pallas import tpu as pltpu
from jax.sharding import PartitionSpec as P

D = 8192
HEAD_DIM = 128
GROUP = 8
WIN = 64


exact_mode = lax.Precision.HIGHEST


def shifted(block, axis, distance):
    devices = range(lax.axis_size(axis))
    route = [(i - distance, i) for i in devices if i - distance in devices]
    return lax.ppermute(block, axis, route)


def taylor_square(features):
    feature_count = features.shape[-1]
    outer = features[..., :, None] * features[..., None, :]
    return outer.reshape(features.shape[:-1] + (feature_count * feature_count,))


def square_grad(grad_square, features):
    feature_count = features.shape[-1]
    matrix = grad_square.reshape(features.shape + (feature_count,))
    return jnp.einsum("...fh,...h->...f", matrix, features, precision=exact_mode) + jnp.einsum(
        "...hf,...h->...f", matrix, features, precision=exact_mode
    )


def exchange_kernel(count, head_count, mode, x_ref, row_ref, out_ref, row_out, buf, row_buf, send, recv, row_send, row_recv):
    me = lax.axis_index("ctx")
    head = lax.axis_index("head")
    mesh_ids = pl.DeviceIdType.MESH
    barrier = pltpu.get_barrier_semaphore()
    for d in range(1, count):
        pl.semaphore_signal(
            barrier, inc=1, device_id=(lax.rem(me + d, count), head), device_id_type=mesh_ids
        )
    for d in range(1, head_count):
        pl.semaphore_signal(
            barrier, inc=1, device_id=(me, lax.rem(head + d, head_count)), device_id_type=mesh_ids
        )
    pl.semaphore_wait(barrier, count + head_count - 2)

    def wanted(source, target):
        return {"lower": source < target, "upper": source > target, "all": source != target}[mode]

    def ctx_copy(d):
        return pltpu.make_async_remote_copy(
            src_ref=x_ref,
            dst_ref=buf.at[me],
            send_sem=send.at[d],
            recv_sem=recv.at[me],
            device_id=(lax.rem(me + d, count), head),
            device_id_type=mesh_ids,
        )

    def row_copy(d):
        return pltpu.make_async_remote_copy(
            src_ref=row_ref,
            dst_ref=row_buf.at[head],
            send_sem=row_send.at[d],
            recv_sem=row_recv.at[head],
            device_id=(me, lax.rem(head + d, head_count)),
            device_id_type=mesh_ids,
        )

    def ctx_arrival(source):
        return pltpu.make_async_remote_copy(
            src_ref=x_ref,
            dst_ref=buf.at[source],
            send_sem=send.at[0],
            recv_sem=recv.at[source],
            device_id=(source, head),
            device_id_type=mesh_ids,
        )

    def row_arrival(source):
        return pltpu.make_async_remote_copy(
            src_ref=row_ref,
            dst_ref=row_buf.at[source],
            send_sem=row_send.at[0],
            recv_sem=row_recv.at[source],
            device_id=(me, source),
            device_id_type=mesh_ids,
        )

    for d in range(1, count):

        @pl.when(wanted(me, lax.rem(me + d, count)))
        def _():
            ctx_copy(d).start()

    for d in range(1, head_count):
        row_copy(d).start()

    row_out[...] = jnp.zeros_like(row_out)
    for source in range(head_count):

        @pl.when(source == head)
        def _():
            row_out[...] += row_ref[...]

        @pl.when(source != head)
        def _():
            row_arrival(source).wait_recv()
            row_out[...] += row_buf[source]

    out_ref[...] = jnp.zeros_like(out_ref)
    for source in range(count):
        if mode == "all":

            @pl.when(source == me)
            def _():
                out_ref[...] += x_ref[...]

        @pl.when(wanted(source, me))
        def _():
            ctx_arrival(source).wait_recv()
            out_ref[...] += buf[source]

    for d in range(1, count):

        @pl.when(wanted(me, lax.rem(me + d, count)))
        def _():
            ctx_copy(d).wait_send()

    for d in range(1, head_count):
        row_copy(d).wait_send()


def exchange(x, row, mode, collective_id):
    count = lax.axis_size("ctx")
    head_count = lax.axis_size("head")
    vmem = pl.BlockSpec(memory_space=pltpu.VMEM)
    return pl.pallas_call(
        functools.partial(exchange_kernel, count, head_count, mode),
        out_shape=(
            jax.ShapeDtypeStruct(x.shape, jnp.float32),
            jax.ShapeDtypeStruct(row.shape, jnp.float32),
        ),
        in_specs=[vmem, vmem],
        out_specs=(vmem, vmem),
        scratch_shapes=[
            pltpu.VMEM((count,) + x.shape, jnp.float32),
            pltpu.VMEM((head_count,) + row.shape, jnp.float32),
            pltpu.SemaphoreType.DMA((count,)),
            pltpu.SemaphoreType.DMA((count,)),
            pltpu.SemaphoreType.DMA((head_count,)),
            pltpu.SemaphoreType.DMA((head_count,)),
        ],
        compiler_params=pltpu.CompilerParams(collective_id=collective_id, has_side_effects=True),
        cost_estimate=pl.CostEstimate(
            flops=count * x.size, bytes_accessed=40 * count * x.size, transcendentals=0
        ),
    )(x, row)


def pack(square, linear, square_den, linear_den, flat):
    groups, feature_count = linear_den.shape
    squares = feature_count * feature_count
    square_rows = square_den.reshape(groups, squares // HEAD_DIM, HEAD_DIM)
    linear_rows = jnp.pad(linear_den, ((0, 0), (0, HEAD_DIM - feature_count)))[:, None]
    small = jnp.concatenate([flat[:, None], linear_rows, square_rows], 1)
    small = jnp.pad(small, ((0, 0), (0, -small.shape[1] % 8), (0, 0)))
    return jnp.concatenate([square, linear, small], 1).reshape(-1, HEAD_DIM)


def unpack(packed, groups, feature_count):
    squares = feature_count * feature_count
    packed = packed.reshape(groups, -1, HEAD_DIM)
    top = squares + feature_count
    square_den = packed[:, top + 2 : top + 2 + squares // HEAD_DIM].reshape(groups, squares)
    return (
        packed[:, :squares],
        packed[:, squares:top],
        square_den,
        packed[:, top + 1, :feature_count],
        packed[:, top],
    )


def ring_gather(block):
    count = lax.axis_size("ctx")
    me = lax.axis_index("ctx")
    rows = block.shape[0]
    half = rows // 2
    ring = list(range(0, count, 2)) + list(range(1, count, 2))[::-1]
    place = [ring.index(i) for i in range(count)]
    position = jnp.array(place, jnp.int32)[me]
    ring_table = jnp.array(ring, jnp.int32)
    up_route = [(ring[p], ring[(p + 1) % count]) for p in range(count)]
    down_route = [(ring[(p + 1) % count], ring[p]) for p in range(count)]
    up, down = block[:half], block[half:]
    pieces = [(me, up, down, me)]
    for step in range(1, count):
        up = lax.ppermute(up, "ctx", up_route)
        down = lax.ppermute(down, "ctx", down_route)
        pieces.append(
            (
                ring_table[(position - step) % count],
                up,
                down,
                ring_table[(position + step) % count],
            )
        )
    return pieces


def assemble(pieces, rows):
    half = rows // 2
    count = len(pieces)
    full = jnp.zeros((count * rows, pieces[0][1].shape[1]), pieces[0][1].dtype)
    for up_owner, up, down, down_owner in pieces:
        full = lax.dynamic_update_slice(full, up, (up_owner * rows, 0))
        full = lax.dynamic_update_slice(full, down, (down_owner * rows + half, 0))
    return full


def flipped(block, bit):
    return lax.ppermute(block, "head", [(i, i ^ bit) for i in range(4)])


def gather_heads(block):
    if lax.axis_size("head") != 4:
        return lax.all_gather(block, "head", axis=1, tiled=True)
    head = lax.axis_index("head")
    rows, width = block.shape
    far = flipped(block, 2)
    near = flipped(block, 1)
    diagonal = flipped(far, 1)
    full = jnp.zeros((rows, 4 * width), block.dtype)
    for bit, member in ((0, block), (2, far), (1, near), (3, diagonal)):
        full = lax.dynamic_update_slice(full, member, (0, (head ^ bit) * width))
    return full


def scatter_heads(d_student, proj_full):
    def product(weights):
        return lax.dot_general(
            d_student, weights, (((1,), (1,)), ((), ())), preferred_element_type=jnp.float32
        ).astype(jnp.bfloat16)

    if lax.axis_size("head") != 4:
        terms = product(proj_full)
        return lax.psum_scatter(terms, "head", scatter_dimension=1, tiled=True).astype(jnp.float32)
    head = lax.axis_index("head")
    width = proj_full.shape[0] // 4

    def block(bit):
        return product(lax.dynamic_slice_in_dim(proj_full, (head ^ bit) * width, width, 0))

    diagonal = flipped(block(3), 1)
    far = block(2)
    pair = (far.astype(jnp.float32) + diagonal.astype(jnp.float32)).astype(jnp.bfloat16)
    far_sum = flipped(pair, 2)
    near = flipped(block(1), 1)
    own = block(0)
    return own.astype(jnp.float32) + near.astype(jnp.float32) + far_sum.astype(jnp.float32)


def window_tiles(extended, tok_rows):
    tile_count = tok_rows // WIN
    first = extended[:tok_rows].reshape((tile_count, WIN) + extended.shape[1:])
    second = extended[WIN:].reshape((tile_count, WIN) + extended.shape[1:])
    return jnp.concatenate([first, second], 1)


def local(queries, keys, values, feature_map, out_proj, teacher):
    tok_rows = queries.shape[0]
    kv_groups = keys.shape[1] // HEAD_DIM
    ctx_count = lax.axis_size("ctx")
    ctx_index = lax.axis_index("ctx")
    pieces = ring_gather(out_proj)
    query_heads = queries.reshape(tok_rows, kv_groups, GROUP, HEAD_DIM)
    key_heads = keys.reshape(tok_rows, kv_groups, HEAD_DIM)
    value_heads = values.reshape(tok_rows, kv_groups, HEAD_DIM)
    value_float = value_heads.astype(jnp.float32)
    query_features = jnp.einsum(
        "tgqe,gef->tgqf", query_heads, feature_map, preferred_element_type=jnp.float32
    )
    key_features = jnp.einsum(
        "tge,gef->tgf", key_heads, feature_map, preferred_element_type=jnp.float32
    )
    rim_rows = shifted(jnp.stack([keys[tok_rows - WIN :], values[tok_rows - WIN :]]), "ctx", 1)
    keys_ext = jnp.concatenate([rim_rows[0], keys], 0).reshape(tok_rows + WIN, kv_groups, HEAD_DIM)
    values_ext = jnp.concatenate([rim_rows[1], values], 0).reshape(
        tok_rows + WIN, kv_groups, HEAD_DIM
    )
    tile_count = tok_rows // WIN
    key_tiles = window_tiles(keys_ext, tok_rows)
    value_tiles = window_tiles(values_ext, tok_rows)
    query_tiles = query_heads.reshape(tile_count, WIN, kv_groups, GROUP, HEAD_DIM)
    scores = jnp.einsum(
        "ntgqe,nsge->ngqts", query_tiles, key_tiles, preferred_element_type=jnp.float32
    ) / math.sqrt(HEAD_DIM)
    tile_pos = lax.broadcasted_iota(jnp.int32, (tile_count, WIN, 2 * WIN), 0)
    query_pos = lax.broadcasted_iota(jnp.int32, (tile_count, WIN, 2 * WIN), 1)
    key_pos = lax.broadcasted_iota(jnp.int32, (tile_count, WIN, 2 * WIN), 2)
    distance = query_pos + WIN - key_pos
    allowed = (
        (distance >= 0)
        & (distance < WIN)
        & (ctx_index * tok_rows + tile_pos * WIN + key_pos - WIN >= 0)
    )
    allowed = allowed[:, None, None]
    scores = jnp.where(allowed, scores, -jnp.inf)
    row_max = jnp.max(scores, axis=-1, keepdims=True)
    weights = jnp.where(allowed, jnp.exp(scores - row_max), 0.0)
    attn_weights = (weights / jnp.sum(weights, axis=-1, keepdims=True)).astype(jnp.bfloat16)
    window_out = jnp.einsum(
        "ngqts,nsge->ntgqe", attn_weights, value_tiles, preferred_element_type=jnp.float32
    ).reshape(tok_rows, kv_groups, GROUP, HEAD_DIM)
    causal = lax.broadcasted_iota(jnp.int32, (tok_rows, tok_rows), 0) >= lax.broadcasted_iota(
        jnp.int32, (tok_rows, tok_rows), 1
    )
    qk_inner = (
        jnp.einsum("tgqf,sgf->gqts", query_features, key_features, precision=exact_mode) / 4.0
    )
    kernel = jnp.where(causal, 1.0 + qk_inner + 0.5 * qk_inner * qk_inner, 0.0)
    numerator = jnp.einsum(
        "gqts,sge->tgqe", kernel.astype(jnp.bfloat16), value_heads, preferred_element_type=jnp.float32
    )
    denominator = jnp.transpose(jnp.sum(kernel, axis=-1), (2, 0, 1))
    key_square = taylor_square(key_features)
    own_square_v = jnp.einsum("sgk,sge->gke", key_square, value_float, precision=exact_mode)
    own_linear_v = jnp.einsum("sgf,sge->gfe", key_features, value_float, precision=exact_mode)
    own_values = jnp.sum(value_float, axis=0)
    own_square_k = jnp.sum(key_square, axis=0)
    own_linear_k = jnp.sum(key_features, axis=0)
    no_row = jnp.zeros((8, HEAD_DIM), jnp.float32)
    packed = pack(own_square_v, own_linear_v, own_square_k, own_linear_k, own_values)
    earlier, _ = exchange(packed, no_row, "lower", 0)
    feature_count = feature_map.shape[2]
    past_square_v, past_linear_v, past_square_k, past_linear_k, past_values = unpack(
        earlier, kv_groups, feature_count
    )
    past_count = (ctx_index * tok_rows).astype(jnp.float32)
    query_square = taylor_square(query_features)
    numerator = (
        numerator
        + jnp.einsum("tgqk,gke->tgqe", query_square, past_square_v, precision=exact_mode) / 32.0
        + jnp.einsum("tgqf,gfe->tgqe", query_features, past_linear_v, precision=exact_mode) / 4.0
        + past_values[None, :, None, :]
    )
    denominator = (
        denominator
        + jnp.einsum("tgqk,gk->tgq", query_square, past_square_k, precision=exact_mode) / 32.0
        + jnp.einsum("tgqf,gf->tgq", query_features, past_linear_k, precision=exact_mode) / 4.0
        + past_count
    )
    linear_out = numerator / denominator[..., None]
    head_out = (
        (linear_out + window_out)
        .astype(jnp.bfloat16)
        .reshape(tok_rows, kv_groups * GROUP * HEAD_DIM)
    )
    all_heads = gather_heads(head_out)
    proj_full = assemble(pieces, out_proj.shape[0])
    projected = jnp.dot(all_heads, proj_full, preferred_element_type=jnp.float32)
    student_out = projected.astype(jnp.bfloat16)
    residual = student_out.astype(jnp.float32) - teacher.astype(jnp.float32)
    total_rows = tok_rows * ctx_count
    squared = jnp.sum(residual * residual)
    d_student = (2.0 * residual / total_rows).astype(jnp.bfloat16)
    head_grad = scatter_heads(d_student, proj_full).reshape(
        tok_rows, kv_groups, GROUP, HEAD_DIM
    )
    numerator_grad = head_grad / denominator[..., None]
    denominator_grad = -jnp.sum(head_grad * linear_out, axis=-1) / denominator
    kernel_grad = (
        jnp.einsum("tgqe,sge->gqts", numerator_grad, value_float, precision=exact_mode)
        + jnp.transpose(denominator_grad, (1, 2, 0))[..., None]
    )
    inner_grad = jnp.where(causal, kernel_grad * (1.0 + qk_inner), 0.0) / 4.0
    query_grad = jnp.einsum("gqts,sgf->tgqf", inner_grad, key_features, precision=exact_mode)
    key_grad = jnp.einsum("gqts,tgqf->sgf", inner_grad, query_features, precision=exact_mode)
    query_square_grad = (
        jnp.einsum("tgqe,gke->tgqk", numerator_grad, past_square_v, precision=exact_mode)
        + denominator_grad[..., None] * past_square_k[None, :, None, :]
    ) / 32.0
    query_grad = (
        query_grad
        + (
            jnp.einsum("tgqe,gfe->tgqf", numerator_grad, past_linear_v, precision=exact_mode)
            + denominator_grad[..., None] * past_linear_k[None, :, None, :]
        )
        / 4.0
        + square_grad(query_square_grad, query_features)
    )
    own_back_square = jnp.einsum(
        "tgqk,tgqe->gke", query_square, numerator_grad, precision=exact_mode
    )
    own_back_linear = jnp.einsum(
        "tgqf,tgqe->gfe", query_features, numerator_grad, precision=exact_mode
    )
    own_den_square = jnp.einsum(
        "tgqk,tgq->gk", query_square, denominator_grad, precision=exact_mode
    )
    own_den_linear = jnp.einsum(
        "tgqf,tgq->gf", query_features, denominator_grad, precision=exact_mode
    )
    packed_back = pack(
        own_back_square,
        own_back_linear,
        own_den_square,
        own_den_linear,
        jnp.zeros((kv_groups, HEAD_DIM), jnp.float32),
    )
    later, loss_row = exchange(
        packed_back, jnp.full((8, HEAD_DIM), squared, jnp.float32), "upper", 1
    )
    later_square, later_linear, later_den_square, later_den_linear, _ = unpack(
        later, kv_groups, feature_count
    )
    key_square_grad = (
        jnp.einsum("gke,sge->sgk", later_square, value_float, precision=exact_mode)
        + later_den_square[None]
    ) / 32.0
    key_grad = (
        key_grad
        + (
            jnp.einsum("gfe,sge->sgf", later_linear, value_float, precision=exact_mode)
            + later_den_linear[None]
        )
        / 4.0
        + square_grad(key_square_grad, key_features)
    )
    own_grad = jnp.einsum(
        "tgqe,tgqf->gef", query_heads.astype(jnp.float32), query_grad, precision=exact_mode
    ) + jnp.einsum("tge,tgf->gef", key_heads.astype(jnp.float32), key_grad, precision=exact_mode)
    packed_grad = jnp.concatenate([own_grad.reshape(-1, HEAD_DIM), loss_row], 0)
    summed, _ = exchange(packed_grad, no_row, "all", 2)
    feature_grad = summed[:-8].reshape(own_grad.shape)
    loss_value = summed[-8, 0] / (total_rows * D)
    return (student_out, loss_value, feature_grad)


def solution(mesh):
    return jax.shard_map(
        local,
        mesh=mesh,
        in_specs=(
            P("ctx", "head"),
            P("ctx", "head"),
            P("ctx", "head"),
            P("head", None, None),
            P("ctx", "head"),
            P("ctx", "head"),
        ),
        out_specs=(P("ctx", "head"), P(), P("head", None, None)),
        check_vma=False,
    )
```

```python
import functools
import math

import jax
import jax.numpy as jnp
from jax import lax
from jax.experimental import pallas as pl
from jax.experimental.pallas import tpu as pltpu
from jax.sharding import PartitionSpec as P

D = 8192
HEAD_DIM = 128
GROUP = 8
WIN = 64


exact_mode = lax.Precision.HIGHEST


def shifted(block, axis, distance):
    devices = range(lax.axis_size(axis))
    route = [(i - distance, i) for i in devices if i - distance in devices]
    return lax.ppermute(block, axis, route)


def taylor_square(features):
    feature_count = features.shape[-1]
    outer = features[..., :, None] * features[..., None, :]
    return outer.reshape(features.shape[:-1] + (feature_count * feature_count,))


def two_terms(x):
    high = lax.reduce_precision(x, 8, 7)
    return jnp.concatenate([high.astype(jnp.bfloat16), (x - high).astype(jnp.bfloat16)], -1)


def joined(pair):
    half = pair.shape[-1] // 2
    return pair[..., :half] + pair[..., half:]


def square_grad(grad_square, features):
    feature_count = features.shape[-1]
    matrix = grad_square.reshape(features.shape + (feature_count,))
    return jnp.einsum("...fh,...h->...f", matrix, features, precision=exact_mode) + jnp.einsum(
        "...hf,...h->...f", matrix, features, precision=exact_mode
    )


def exchange_kernel(count, head_count, mode, x_ref, row_ref, out_ref, row_out, buf, row_buf, send, recv, row_send, row_recv):
    me = lax.axis_index("ctx")
    head = lax.axis_index("head")
    mesh_ids = pl.DeviceIdType.MESH
    barrier = pltpu.get_barrier_semaphore()
    for d in range(1, count):
        pl.semaphore_signal(
            barrier, inc=1, device_id=(lax.rem(me + d, count), head), device_id_type=mesh_ids
        )
    for d in range(1, head_count):
        pl.semaphore_signal(
            barrier, inc=1, device_id=(me, lax.rem(head + d, head_count)), device_id_type=mesh_ids
        )
    pl.semaphore_wait(barrier, count + head_count - 2)

    def wanted(source, target):
        return {"lower": source < target, "upper": source > target, "all": source != target}[mode]

    def ctx_copy(d):
        return pltpu.make_async_remote_copy(
            src_ref=x_ref,
            dst_ref=buf.at[me],
            send_sem=send.at[d],
            recv_sem=recv.at[me],
            device_id=(lax.rem(me + d, count), head),
            device_id_type=mesh_ids,
        )

    def row_copy(d):
        return pltpu.make_async_remote_copy(
            src_ref=row_ref,
            dst_ref=row_buf.at[head],
            send_sem=row_send.at[d],
            recv_sem=row_recv.at[head],
            device_id=(me, lax.rem(head + d, head_count)),
            device_id_type=mesh_ids,
        )

    def ctx_arrival(source):
        return pltpu.make_async_remote_copy(
            src_ref=x_ref,
            dst_ref=buf.at[source],
            send_sem=send.at[0],
            recv_sem=recv.at[source],
            device_id=(source, head),
            device_id_type=mesh_ids,
        )

    def row_arrival(source):
        return pltpu.make_async_remote_copy(
            src_ref=row_ref,
            dst_ref=row_buf.at[source],
            send_sem=row_send.at[0],
            recv_sem=row_recv.at[source],
            device_id=(me, source),
            device_id_type=mesh_ids,
        )

    for d in range(1, count):

        @pl.when(wanted(me, lax.rem(me + d, count)))
        def _():
            ctx_copy(d).start()

    for d in range(1, head_count):
        row_copy(d).start()

    row_out[...] = jnp.zeros_like(row_out)
    for source in range(head_count):

        @pl.when(source == head)
        def _():
            row_out[...] += row_ref[...]

        @pl.when(source != head)
        def _():
            row_arrival(source).wait_recv()
            row_out[...] += row_buf[source]

    out_ref[...] = jnp.zeros_like(out_ref)
    for source in range(count):
        if mode == "all":

            @pl.when(source == me)
            def _():
                out_ref[...] += x_ref[...].astype(jnp.float32)

        @pl.when(wanted(source, me))
        def _():
            ctx_arrival(source).wait_recv()
            out_ref[...] += buf[source].astype(jnp.float32)

    for d in range(1, count):

        @pl.when(wanted(me, lax.rem(me + d, count)))
        def _():
            ctx_copy(d).wait_send()

    for d in range(1, head_count):
        row_copy(d).wait_send()


def exchange(x, row, mode, collective_id):
    count = lax.axis_size("ctx")
    head_count = lax.axis_size("head")
    vmem = pl.BlockSpec(memory_space=pltpu.VMEM)
    return pl.pallas_call(
        functools.partial(exchange_kernel, count, head_count, mode),
        out_shape=(
            jax.ShapeDtypeStruct(x.shape, jnp.float32),
            jax.ShapeDtypeStruct(row.shape, jnp.float32),
        ),
        in_specs=[vmem, vmem],
        out_specs=(vmem, vmem),
        scratch_shapes=[
            pltpu.VMEM((count,) + x.shape, x.dtype),
            pltpu.VMEM((head_count,) + row.shape, jnp.float32),
            pltpu.SemaphoreType.DMA((count,)),
            pltpu.SemaphoreType.DMA((count,)),
            pltpu.SemaphoreType.DMA((head_count,)),
            pltpu.SemaphoreType.DMA((head_count,)),
        ],
        compiler_params=pltpu.CompilerParams(collective_id=collective_id, has_side_effects=True),
        cost_estimate=pl.CostEstimate(
            flops=count * x.size, bytes_accessed=40 * count * x.size, transcendentals=0
        ),
    )(x, row)


def pack(square, linear, square_den, linear_den, flat):
    groups, feature_count = linear_den.shape
    squares = feature_count * feature_count
    square_rows = square_den.reshape(groups, squares // HEAD_DIM, HEAD_DIM)
    linear_rows = jnp.pad(linear_den, ((0, 0), (0, HEAD_DIM - feature_count)))[:, None]
    small = jnp.concatenate([flat[:, None], linear_rows, square_rows], 1)
    small = jnp.pad(small, ((0, 0), (0, -small.shape[1] % 16), (0, 0)))
    return jnp.concatenate([square, linear, small], 1).reshape(-1, HEAD_DIM)


def unpack(packed, groups, feature_count):
    squares = feature_count * feature_count
    packed = packed.reshape(groups, -1, HEAD_DIM)
    top = squares + feature_count
    square_den = packed[:, top + 2 : top + 2 + squares // HEAD_DIM].reshape(groups, squares)
    return (
        packed[:, :squares],
        packed[:, squares:top],
        square_den,
        packed[:, top + 1, :feature_count],
        packed[:, top],
    )


def ring_gather(block):
    count = lax.axis_size("ctx")
    me = lax.axis_index("ctx")
    rows = block.shape[0]
    half = rows // 2
    ring = list(range(0, count, 2)) + list(range(1, count, 2))[::-1]
    place = [ring.index(i) for i in range(count)]
    position = jnp.array(place, jnp.int32)[me]
    ring_table = jnp.array(ring, jnp.int32)
    up_route = [(ring[p], ring[(p + 1) % count]) for p in range(count)]
    down_route = [(ring[(p + 1) % count], ring[p]) for p in range(count)]
    up, down = block[:half], block[half:]
    pieces = [(me, up, down, me)]
    for step in range(1, count):
        up = lax.ppermute(up, "ctx", up_route)
        down = lax.ppermute(down, "ctx", down_route)
        pieces.append(
            (
                ring_table[(position - step) % count],
                up,
                down,
                ring_table[(position + step) % count],
            )
        )
    return pieces


def after_hop(pieces, hop, *members):
    if hop >= len(pieces):
        return members
    up_owner, up, down, down_owner = pieces[hop]
    up, down, *members = lax.optimization_barrier((up, down, *members))
    pieces[hop] = (up_owner, up, down, down_owner)
    return members


def assemble(pieces, zero, rows):
    half = rows // 2
    count = len(pieces)
    full = jnp.broadcast_to(zero, (count * rows, pieces[0][1].shape[1]))
    for up_owner, up, down, down_owner in pieces:
        full = lax.dynamic_update_slice(full, up, (up_owner * rows, 0))
        full = lax.dynamic_update_slice(full, down, (down_owner * rows + half, 0))
    return full


def flipped(block, bit):
    return lax.ppermute(block, "head", [(i, i ^ bit) for i in range(4)])


def sum_heads(row):
    if lax.axis_size("head") != 4:
        return lax.psum(row, "head")
    row = row + flipped(row, 1)
    return row + flipped(row, 2)


def sum_from(block, sign):
    count = lax.axis_size("ctx")
    devices = range(count)
    total = jnp.zeros_like(block)
    for distance in range(1, count):
        route = [(i, i + sign * distance) for i in devices if i + sign * distance in devices]
        total = total + lax.ppermute(block, "ctx", route)
    return total


def gather_heads(block):
    if lax.axis_size("head") != 4:
        return lax.all_gather(block, "head", axis=1, tiled=True)
    head = lax.axis_index("head")
    rows, width = block.shape
    far = flipped(block, 2)
    near = flipped(block, 1)
    diagonal = flipped(far, 1)
    full = jnp.zeros((rows, 4 * width), block.dtype)
    for bit, member in ((0, block), (2, far), (1, near), (3, diagonal)):
        full = lax.dynamic_update_slice(full, member, (0, (head ^ bit) * width))
    return full


def scatter_heads(d_student, proj_full):
    def product(weights):
        return lax.dot_general(
            d_student, weights, (((1,), (1,)), ((), ())), preferred_element_type=jnp.float32
        ).astype(jnp.bfloat16)

    if lax.axis_size("head") != 4:
        terms = product(proj_full)
        return lax.psum_scatter(terms, "head", scatter_dimension=1, tiled=True).astype(jnp.float32)
    head = lax.axis_index("head")
    width = proj_full.shape[0] // 4

    def block(bit):
        return product(lax.dynamic_slice_in_dim(proj_full, (head ^ bit) * width, width, 0))

    diagonal = flipped(block(3), 1)
    far = block(2)
    pair = (far.astype(jnp.float32) + diagonal.astype(jnp.float32)).astype(jnp.bfloat16)
    far_sum = flipped(pair, 2)
    near = flipped(block(1), 1)
    own = block(0)
    return own.astype(jnp.float32) + near.astype(jnp.float32) + far_sum.astype(jnp.float32)


def window_tiles(extended, tok_rows):
    tile_count = tok_rows // WIN
    first = extended[:tok_rows].reshape((tile_count, WIN) + extended.shape[1:])
    second = extended[WIN:].reshape((tile_count, WIN) + extended.shape[1:])
    return jnp.concatenate([first, second], 1)


def local(queries, keys, values, feature_map, out_proj, teacher):
    tok_rows = queries.shape[0]
    kv_groups = keys.shape[1] // HEAD_DIM
    ctx_count = lax.axis_size("ctx")
    ctx_index = lax.axis_index("ctx")
    pieces = ring_gather(out_proj)
    query_heads = queries.reshape(tok_rows, kv_groups, GROUP, HEAD_DIM)
    key_heads = keys.reshape(tok_rows, kv_groups, HEAD_DIM)
    value_heads = values.reshape(tok_rows, kv_groups, HEAD_DIM)
    value_float = value_heads.astype(jnp.float32)
    query_features = jnp.einsum(
        "tgqe,gef->tgqf", query_heads, feature_map, preferred_element_type=jnp.float32
    )
    key_features = jnp.einsum(
        "tge,gef->tgf", key_heads, feature_map, preferred_element_type=jnp.float32
    )
    rim_rows = shifted(jnp.stack([keys[tok_rows - WIN :], values[tok_rows - WIN :]]), "ctx", 1)
    keys_ext = jnp.concatenate([rim_rows[0], keys], 0).reshape(tok_rows + WIN, kv_groups, HEAD_DIM)
    values_ext = jnp.concatenate([rim_rows[1], values], 0).reshape(
        tok_rows + WIN, kv_groups, HEAD_DIM
    )
    tile_count = tok_rows // WIN
    key_tiles = window_tiles(keys_ext, tok_rows)
    value_tiles = window_tiles(values_ext, tok_rows)
    query_tiles = query_heads.reshape(tile_count, WIN, kv_groups, GROUP, HEAD_DIM)
    causal = lax.broadcasted_iota(jnp.int32, (tok_rows, tok_rows), 0) >= lax.broadcasted_iota(
        jnp.int32, (tok_rows, tok_rows), 1
    )
    qk_inner = (
        jnp.einsum("tgqf,sgf->gqts", query_features, key_features, precision=exact_mode) / 4.0
    )
    kernel = jnp.where(causal, 1.0 + qk_inner + 0.5 * qk_inner * qk_inner, 0.0)
    numerator = jnp.einsum(
        "gqts,sge->tgqe", kernel.astype(jnp.bfloat16), value_heads, preferred_element_type=jnp.float32
    )
    denominator = jnp.transpose(jnp.sum(kernel, axis=-1), (2, 0, 1))
    query_tiles, numerator, denominator = after_hop(
        pieces, 1, query_tiles, numerator, denominator
    )
    scores = jnp.einsum(
        "ntgqe,nsge->ngqts", query_tiles, key_tiles, preferred_element_type=jnp.float32
    ) / math.sqrt(HEAD_DIM)
    tile_pos = lax.broadcasted_iota(jnp.int32, (tile_count, WIN, 2 * WIN), 0)
    query_pos = lax.broadcasted_iota(jnp.int32, (tile_count, WIN, 2 * WIN), 1)
    key_pos = lax.broadcasted_iota(jnp.int32, (tile_count, WIN, 2 * WIN), 2)
    distance = query_pos + WIN - key_pos
    allowed = (
        (distance >= 0)
        & (distance < WIN)
        & (ctx_index * tok_rows + tile_pos * WIN + key_pos - WIN >= 0)
    )
    allowed = allowed[:, None, None]
    scores = jnp.where(allowed, scores, -jnp.inf)
    row_max = jnp.max(scores, axis=-1, keepdims=True)
    weights = jnp.where(allowed, jnp.exp(scores - row_max), 0.0)
    attn_weights = (weights / jnp.sum(weights, axis=-1, keepdims=True)).astype(jnp.bfloat16)
    window_out = jnp.einsum(
        "ngqts,nsge->ntgqe", attn_weights, value_tiles, preferred_element_type=jnp.float32
    ).reshape(tok_rows, kv_groups, GROUP, HEAD_DIM)
    key_square = taylor_square(key_features)
    own_square_v = jnp.einsum("sgk,sge->gke", key_square, value_float, precision=exact_mode)
    own_linear_v = jnp.einsum("sgf,sge->gfe", key_features, value_float, precision=exact_mode)
    own_values = jnp.sum(value_float, axis=0)
    own_square_k = jnp.sum(key_square, axis=0)
    own_linear_k = jnp.sum(key_features, axis=0)
    no_row = jnp.zeros((8, HEAD_DIM), jnp.float32)
    packed = pack(own_square_v, own_linear_v, own_square_k, own_linear_k, own_values)
    earlier, window_out = after_hop(pieces, 2, sum_from(packed, 1), window_out)
    feature_count = feature_map.shape[2]
    past_square_v, past_linear_v, past_square_k, past_linear_k, past_values = unpack(
        earlier, kv_groups, feature_count
    )
    past_count = (ctx_index * tok_rows).astype(jnp.float32)
    query_square = taylor_square(query_features)
    numerator = (
        numerator
        + jnp.einsum("tgqk,gke->tgqe", query_square, past_square_v, precision=exact_mode) / 32.0
        + jnp.einsum("tgqf,gfe->tgqe", query_features, past_linear_v, precision=exact_mode) / 4.0
        + past_values[None, :, None, :]
    )
    denominator = (
        denominator
        + jnp.einsum("tgqk,gk->tgq", query_square, past_square_k, precision=exact_mode) / 32.0
        + jnp.einsum("tgqf,gf->tgq", query_features, past_linear_k, precision=exact_mode) / 4.0
        + past_count
    )
    linear_out = numerator / denominator[..., None]
    head_out = (
        (linear_out + window_out)
        .astype(jnp.bfloat16)
        .reshape(tok_rows, kv_groups * GROUP * HEAD_DIM)
    )
    head_out, zero = after_hop(pieces, 3, head_out, jnp.zeros((), jnp.bfloat16))
    all_heads = gather_heads(head_out)
    proj_full = assemble(pieces, zero, out_proj.shape[0])
    projected = jnp.dot(all_heads, proj_full, preferred_element_type=jnp.float32)
    student_out = projected.astype(jnp.bfloat16)
    residual = student_out.astype(jnp.float32) - teacher.astype(jnp.float32)
    total_rows = tok_rows * ctx_count
    squared = jnp.sum(residual * residual)
    d_student = (2.0 * residual / total_rows).astype(jnp.bfloat16)
    head_grad = scatter_heads(d_student, proj_full).reshape(
        tok_rows, kv_groups, GROUP, HEAD_DIM
    )
    numerator_grad = head_grad / denominator[..., None]
    denominator_grad = -jnp.sum(head_grad * linear_out, axis=-1) / denominator
    kernel_grad = (
        jnp.einsum(
            "tgqe,sge->gqts",
            two_terms(numerator_grad),
            jnp.concatenate([value_heads, value_heads], -1),
            preferred_element_type=jnp.float32,
        )
        + jnp.transpose(denominator_grad, (1, 2, 0))[..., None]
    )
    inner_grad = (jnp.where(causal, kernel_grad * (1.0 + qk_inner), 0.0) / 4.0).astype(
        jnp.bfloat16
    )
    query_grad = joined(
        jnp.einsum(
            "gqts,sgf->tgqf",
            inner_grad,
            two_terms(key_features),
            preferred_element_type=jnp.float32,
        )
    )
    key_grad = joined(
        jnp.einsum(
            "gqts,tgqf->sgf",
            inner_grad,
            two_terms(query_features),
            preferred_element_type=jnp.float32,
        )
    )
    query_square_grad = (
        jnp.einsum("tgqe,gke->tgqk", numerator_grad, past_square_v, precision=exact_mode)
        + denominator_grad[..., None] * past_square_k[None, :, None, :]
    ) / 32.0
    query_grad = (
        query_grad
        + (
            jnp.einsum("tgqe,gfe->tgqf", numerator_grad, past_linear_v, precision=exact_mode)
            + denominator_grad[..., None] * past_linear_k[None, :, None, :]
        )
        / 4.0
        + square_grad(query_square_grad, query_features)
    )
    own_back_square = jnp.einsum(
        "tgqk,tgqe->gke", query_square, numerator_grad, precision=exact_mode
    )
    own_back_linear = jnp.einsum(
        "tgqf,tgqe->gfe", query_features, numerator_grad, precision=exact_mode
    )
    own_den_square = jnp.einsum(
        "tgqk,tgq->gk", query_square, denominator_grad, precision=exact_mode
    )
    own_den_linear = jnp.einsum(
        "tgqf,tgq->gf", query_features, denominator_grad, precision=exact_mode
    )
    packed_back = pack(
        own_back_square,
        own_back_linear,
        own_den_square,
        own_den_linear,
        jnp.zeros((kv_groups, HEAD_DIM), jnp.float32),
    )
    later = sum_from(packed_back, -1)
    loss_row = sum_heads(jnp.full((8, HEAD_DIM), squared, jnp.float32))
    later_square, later_linear, later_den_square, later_den_linear, _ = unpack(
        later, kv_groups, feature_count
    )
    key_square_grad = (
        jnp.einsum("gke,sge->sgk", later_square, value_float, precision=exact_mode)
        + later_den_square[None]
    ) / 32.0
    key_grad = (
        key_grad
        + (
            jnp.einsum("gfe,sge->sgf", later_linear, value_float, precision=exact_mode)
            + later_den_linear[None]
        )
        / 4.0
        + square_grad(key_square_grad, key_features)
    )
    own_grad = jnp.einsum(
        "tgqe,tgqf->gef", query_heads.astype(jnp.float32), query_grad, precision=exact_mode
    ) + jnp.einsum("tge,tgf->gef", key_heads.astype(jnp.float32), key_grad, precision=exact_mode)
    packed_grad = jnp.concatenate([own_grad.reshape(-1, HEAD_DIM), loss_row], 0)
    summed, _ = exchange(packed_grad, no_row, "all", 0)
    feature_grad = summed[:-8].reshape(own_grad.shape)
    loss_value = summed[-8, 0] / (total_rows * D)
    return (student_out, loss_value, feature_grad)


def solution(mesh):
    return jax.shard_map(
        local,
        mesh=mesh,
        in_specs=(
            P("ctx", "head"),
            P("ctx", "head"),
            P("ctx", "head"),
            P("head", None, None),
            P("ctx", "head"),
            P("ctx", "head"),
        ),
        out_specs=(P("ctx", "head"), P(), P("head", None, None)),
        check_vma=False,
    )
```
